512 devices in a mesh: row: 16 (over y, x_hi, core), col: 32 (over x_lo, z).
Axes of the slice: x: 4 (x_hi: 2, x_lo: 2; x = x_hi * 2 + x_lo), y: 4, z: 16, core: 2. Of those that a mesh axis runs over, the one named last changes fastest.
Arguments:
- factors: float32 [2, 96, 49152], P(None, 'row', 'col'), may hold values from -0.3125 to 0.3125
- covariance: float32 [12288, 12288], P('row', 'col'), may hold values from -26 to 26, as said below
- noise: float32 [12288, 12288], P('row', 'col'), may hold values from -2.4 to 2.4
- positions: float32 [12288], replicated, may hold values from 0 to 1
Outputs:
- forecast: float32 [12288, 12288], P('row', 'col')
The draws below stay inside these ranges and needn't reach their ends.
Inputs may be any that keep to these rules, and one draw needn't show every extreme that they name: covariance is symmetric, with 2 added on its diagonal.
All inputs are finite; a program needn't handle non-finite values.
Results may differ from the reference program's by a relative error of at most 0.00014.
Values sent between devices are 32-bit elements; how exact they have to be, the bound alone decides.
No kernel may reach another device: no remote copies, remote signals or barrier semaphores. Data moves between devices by JAX's collectives and lax.ppermute only.
A program may use at most 64 MiB of HBM per device.

```python
import jax
import jax.numpy as jnp
from jax import lax

N = 12288
B = 128
NB = 96


def draw_covariance(key, part):
    first = jax.random.fold_in(key, 0)
    drawn = jax.random.normal(first, (N, N), jnp.float32)
    drawn = jnp.clip(drawn, -6.0, 6.0)
    symmetric = (drawn + drawn.T) * 0.5
    return symmetric + 2.0 * jnp.eye(N, dtype=jnp.float32)


def levels(rng, dims, pieces, least, largest):
    def one(dim, parts):
        steps = jax.random.uniform(jax.random.fold_in(jax.random.fold_in(rng, 6), dim), (parts,), jnp.float32, least / len(pieces), largest / len(pieces))
        return jnp.repeat(jnp.exp(steps), dims[dim] // parts).reshape((-1,) + (1,) * (len(dims) - dim - 1))

    factor_of = one(*pieces[0])
    for cut in pieces[1:]:
        factor_of = factor_of * one(*cut)
    return factor_of


def centred(key, extent, scale, bound, cuts=(), kind=jnp.bfloat16):
    factor_of = levels(key, extent, cuts, -0.22, 0.18) if cuts else 1.0
    drawn = jax.random.normal(key, extent, jnp.float32) * scale * factor_of
    return jnp.minimum(jnp.maximum(drawn, -bound), bound).astype(kind)


def setup_inputs(seed: int = 0) -> dict:
    keys = jax.random.split(jax.random.key(seed), 5)
    factors = centred(keys[0], (2, NB, 3 * B * B), (3 * B) ** -0.5, 0.3125, ((1, 16), (2, 32)), jnp.float32)
    covariance = draw_covariance(jax.random.fold_in(keys[4], 71), 0)
    noise = centred(keys[2], (N, N), 0.3, 2.4, ((0, 16), (1, 32)), jnp.float32)
    positions = jnp.clip(jax.random.uniform(keys[3], (N,), jnp.float32, 0.0, 1.0), 0.0, 1.0)
    return dict(factors=factors, covariance=covariance, noise=noise, positions=positions)


def left_apply(blocks, matrix):
    count = blocks.shape[0]
    size = blocks.shape[2]
    width = matrix.shape[1]
    split = matrix.reshape(count, size, width)
    zero = jnp.zeros((1, size, width), jnp.float32)
    before = jnp.concatenate([zero, split[:-1]], axis=0)
    after = jnp.concatenate([split[1:], zero], axis=0)
    total = jnp.einsum("iab,ibk->iak", blocks[:, 0], before, precision=lax.Precision.HIGHEST)
    total = total + jnp.einsum("iab,ibk->iak", blocks[:, 1], split, precision=lax.Precision.HIGHEST)
    total = total + jnp.einsum("iab,ibk->iak", blocks[:, 2], after, precision=lax.Precision.HIGHEST)
    return total.reshape(count * size, width)


def right_apply(blocks, matrix):
    count = blocks.shape[0]
    size = blocks.shape[2]
    height = matrix.shape[0]
    split = matrix.reshape(height, count, size)
    zero = jnp.zeros((height, 1, size), jnp.float32)
    before = jnp.concatenate([zero, split[:, :-1]], axis=1)
    after = jnp.concatenate([split[:, 1:], zero], axis=1)
    total = jnp.einsum("kib,iab->kia", before, blocks[:, 0], precision=lax.Precision.HIGHEST)
    total = total + jnp.einsum("kib,iab->kia", split, blocks[:, 1], precision=lax.Precision.HIGHEST)
    total = total + jnp.einsum("kib,iab->kia", after, blocks[:, 2], precision=lax.Precision.HIGHEST)
    return total.reshape(height, count * size)


def reference(factors, covariance, noise, positions):
    shaped = factors.reshape(2, NB, 3, B, B)
    moved = left_apply(shaped[0], covariance)
    moved = left_apply(shaped[1], moved)
    spread = right_apply(shaped[0], moved)
    spread = right_apply(shaped[1], spread)
    distance = (positions[:, None] - positions[None, :]) / 0.5
    taper = jnp.exp(-distance * distance)
    return spread * taper + noise
```

```python
import jax
import jax.numpy as jnp
from jax import lax
from jax.experimental import pallas as pl
from jax.experimental.pallas import tpu as pltpu
from jax.sharding import PartitionSpec as P

B = 128
T = 12
XL, Z = 2, 16
Y, XH, CORE = 4, 2, 2
ROWS, COLS = Y * XH * CORE, XL * Z
BOTH = ("row", "col")
FAR = (0, -4, 4, 8)
NEAR = (0, -1, 1, -2)
YS = (0, -1, 1, 2)


def move(x, target):
    pairs = []
    for r in range(ROWS):
        for c in range(COLS):
            to = target(r, c)
            if to is not None:
                pairs.append((r * COLS + c, to[0] * COLS + to[1]))
    return lax.ppermute(x, BOTH, pairs)


def split_row(r):
    return r // (XH * CORE), (r // CORE) % XH, r % CORE


def row_of(y, xh, core):
    return (y * XH + xh) * CORE + core


def shift_row(x, d):
    return move(x, lambda r, c: (r + d, c) if 0 <= r + d < ROWS else None)


def shift_col(x, d):
    return move(x, lambda r, c: (r, c + d) if 0 <= c + d < COLS else None)


def shift_z(x, d):
    return move(x, lambda r, c: (r, c // Z * Z + (c % Z + d) % Z))


def shift_y(x, d):
    def target(r, c):
        y, xh, core = split_row(r)
        return row_of((y + d) % Y, xh, core), c

    return move(x, target)


def flip_xl(x):
    return move(x, lambda r, c: (r, (c + Z) % COLS))


def flip_core(x):
    return move(x, lambda r, c: (r ^ 1, c))


def turn(x):
    def target(r, c):
        xl, z = divmod(c, Z)
        zh, zl = divmod(z, 4)
        return row_of(zl, zh // 2, xl), 2 * r + zh % 2

    return move(x, target)


def split(x):
    hi = x.astype(jnp.bfloat16)
    return hi, (x - hi.astype(jnp.float32)).astype(jnp.bfloat16)


def product(a, b, contract):
    dims = (contract, ((), ()))
    ah, al = split(a)
    bh, bl = split(b)
    out = lax.dot_general(al, bh, dims, preferred_element_type=jnp.float32)
    out += lax.dot_general(ah, bl, dims, preferred_element_type=jnp.float32)
    return out + lax.dot_general(ah, bh, dims, preferred_element_type=jnp.float32)


def wide(ref, q):
    return jnp.concatenate([ref[q, k * B : (k + 1) * B, :] for k in range(3)], axis=1)


def place(held, piece, slot, at, count):
    start = pl.multiple_of(at * T, 4)
    for q in range(count):
        held[q, pl.ds(start, T), :] = piece[slot, q * T : (q + 1) * T, :]


def right_kernel(spot, mine, other, tile, before, after, out, held, middle):
    y, xh, core, c = spot[0], spot[1], spot[2], spot[3]
    for source, half in ((mine, core), (other, 1 - core)):
        for i, dy in enumerate(YS):
            base = (2 * xh + c % 2) * 4 + (y + dy + Y) % Y
            for j, dz in enumerate(FAR):
                place(held, source, i * 4 + j, half * Z + (base + dz + Z) % Z, 8)
    whole = jnp.concatenate([before[...], tile[...], after[...]], axis=1)
    for j in range(5):
        window = whole[:, j * B : (j + 3) * B]
        middle[:, j * B : (j + 1) * B] = product(window, wide(held, j), ((1,), (1,)))
    for j in range(3):
        window = middle[:, j * B : (j + 3) * B]
        out[:, j * B : (j + 1) * B] = product(window, wide(held, 5 + j), ((1,), (1,)))


def left_kernel(spot, m0, m1, m2, m3, o0, o1, o2, o3, tile, before, after, noise, down, across, out, held, middle):
    xl, z = spot[4], spot[5]
    for sources, half in (((m0, m1, m2, m3), xl), ((o0, o1, o2, o3), 1 - xl)):
        for source, near in zip(sources, NEAR):
            for j, far in enumerate(FAR):
                place(held, source, j, half * Z + (z + near + far + Z) % Z, 14)
    whole = jnp.concatenate([before[...], tile[...], after[...]], axis=0)
    for i in range(8):
        window = whole[i * B : (i + 3) * B, :]
        middle[i * B : (i + 1) * B, :] = product(wide(held, i), window, ((1,), (0,)))
    for i in range(6):
        rows = slice(i * B, (i + 1) * B)
        window = middle[i * B : (i + 3) * B, :]
        spread = product(wide(held, 8 + i), window, ((1,), (0,)))
        distance = (down[rows, :] - across[...]) / 0.5
        out[rows, :] = spread * jnp.exp(-distance * distance) + noise[rows, :]


def local(kernel, count, out, scratch, cost):
    vmem = pl.BlockSpec(memory_space=pltpu.VMEM)
    return pl.pallas_call(
        kernel,
        out_shape=jax.ShapeDtypeStruct(out, jnp.float32),
        in_specs=[pl.BlockSpec(memory_space=pltpu.SMEM)] + [vmem] * count,
        out_specs=vmem,
        scratch_shapes=[pltpu.VMEM(s, jnp.float32) for s in scratch],
        cost_estimate=pl.CostEstimate(flops=cost, bytes_accessed=8 << 20, transcendentals=0),
    )


def body(factors, covariance, noise, positions):
    height, width = covariance.shape
    row, col = lax.axis_index("row"), lax.axis_index("col")
    y, xh, core = row // (XH * CORE), (row // CORE) % XH, row % CORE
    xl, z = col // Z, col % Z
    spot = jnp.stack([y, xh, core, col, xl, z]).astype(jnp.int32)

    pieces = factors.reshape(2, 6, T, B)
    above = shift_row(pieces[0, 5], 1)
    below = shift_row(pieces[0, 0], -1)
    left = shift_col(covariance[:, width - 2 * B :], 1)
    right = shift_col(covariance[:, : 2 * B], -1)
    own = jnp.concatenate([above[None], pieces[0], below[None], pieces[1]], axis=0).reshape(14 * T, B)

    far = jnp.stack([own] + [shift_z(own, -d) for d in FAR[1:]])

    chosen = (z // 4) % 2
    def half(h):
        return jnp.concatenate([far[:, 3 * h * T : (3 * h + 5) * T], far[:, (8 + 3 * h) * T : (11 + 3 * h) * T]], axis=1)
    turned = turn(jnp.where(chosen == 1, half(1), half(0)))
    mine = jnp.concatenate([turned] + [shift_y(turned, -d) for d in YS[1:]])
    other = flip_core(mine)

    near = [far] + [shift_z(far, -d) for d in NEAR[1:]]
    cross = [flip_xl(x) for x in near]

    moved = local(right_kernel, 5, (height, width), [(8, 3 * B, B), (height, 5 * B)], 2000000000)(
        spot, mine, other, covariance, left, right
    )
    before = shift_row(moved[height - 2 * B :], 1)
    after = shift_row(moved[: 2 * B], -1)

    down = lax.dynamic_slice_in_dim(positions, row * height, height, 0).reshape(height, 1)
    across = lax.dynamic_slice_in_dim(positions, col * width, width, 0).reshape(1, width)
    return local(left_kernel, 14, (height, width), [(14, 3 * B, B), (8 * B, width)], 2000000000)(
        spot, *near, *cross, moved, before, after, noise, down, across
    )


def solution(mesh):
    placed = (P(None, "row", "col"), P("row", "col"), P("row", "col"), P())
    return jax.shard_map(body, mesh=mesh, in_specs=placed, out_specs=P("row", "col"), check_vma=False)
```

```python
import jax
import jax.numpy as jnp
from jax import lax
from jax.experimental import pallas as pl
from jax.experimental.pallas import tpu as pltpu
from jax.sharding import PartitionSpec as P

B = 128
T = 12
XL, Z = 2, 16
Y, XH, CORE = 4, 2, 2
ROWS, COLS = Y * XH * CORE, XL * Z
BOTH = ("row", "col")
FAR = (-6, -2, 2, 6)
NEAR = (0, -1, 1, -2)


def move(x, target):
    pairs = []
    for r in range(ROWS):
        for c in range(COLS):
            to = target(r, c)
            if to is not None:
                pairs.append((r * COLS + c, to[0] * COLS + to[1]))
    return lax.ppermute(x, BOTH, pairs)


def odd_pair(i, count):
    j = i + 1 if i % 2 else i - 1
    return j if 0 <= j < count else None


def swap_rows(x, odd):
    def target(r, c):
        to = odd_pair(r, ROWS) if odd else r ^ 1
        return None if to is None else (to, c)

    return move(x, target)


def swap_cols(x, odd):
    def target(r, c):
        to = odd_pair(c, COLS) if odd else c ^ 1
        return None if to is None else (r, to)

    return move(x, target)


def shift_z(x, d):
    return move(x, lambda r, c: (r, c // Z * Z + (c % Z + d) % Z))


def shift_near(x, d):
    return move(x, lambda r, c: (r, c // Z * Z + (c % Z + (d if r % 2 == 0 else -d)) % Z))


def flip_row(x, bit):
    return move(x, lambda r, c: (r ^ bit, c))


def flip_xl(x):
    return move(x, lambda r, c: (r, (c + Z) % COLS))


def turn(x):
    return move(x, lambda r, c: (c // 2, 2 * r + c % 2))


def split(x):
    hi = x.astype(jnp.bfloat16)
    return hi, (x - hi.astype(jnp.float32)).astype(jnp.bfloat16)


def product(a, b, contract):
    dims = (contract, ((), ()))
    ah, al = split(a)
    bh, bl = split(b)
    out = lax.dot_general(al, bh, dims, preferred_element_type=jnp.float32)
    out += lax.dot_general(ah, bl, dims, preferred_element_type=jnp.float32)
    return out + lax.dot_general(ah, bh, dims, preferred_element_type=jnp.float32)


def wide(ref, q):
    return jnp.concatenate([ref[q, k * B : (k + 1) * B, :] for k in range(3)], axis=1)


def place(held, piece, slot, at, count):
    start = pl.multiple_of(at * T, 4)
    for q in range(count):
        held[q, pl.ds(start, T), :] = piece[slot, q * T : (q + 1) * T, :]


def spread_kernel(factors, base, first, second):
    core = lax.axis_index("row") % 2
    base[0:T, :] = jnp.zeros((T, B), jnp.float32)
    base[7 * T : 8 * T, :] = jnp.zeros((T, B), jnp.float32)
    for f, at in ((0, 1), (1, 8)):
        for t in range(T):
            base[pl.ds(at * T + t, 6, stride=T), :] = factors[f, :, t * B : (t + 1) * B]
    top, bottom = base[T : 2 * T, :], base[6 * T : 7 * T, :]

    @pl.when(core == 0)
    def _():
        first[...] = bottom
        second[...] = top

    @pl.when(core == 1)
    def _():
        first[...] = top
        second[...] = bottom


def halves_kernel(base, first, second, own, keep, send):
    core, odd = lax.axis_index("row") % 2, lax.axis_index("col") % 2
    own[...] = base[...]

    @pl.when(core == 0)
    def _():
        own[0:T, :] = second[...]
        own[7 * T : 8 * T, :] = first[...]

    @pl.when(core == 1)
    def _():
        own[0:T, :] = first[...]
        own[7 * T : 8 * T, :] = second[...]

    def half(h, out):
        out[0 : 5 * T, :] = own[3 * h * T : (3 * h + 5) * T, :]
        out[5 * T : 8 * T, :] = own[(8 + 3 * h) * T : (11 + 3 * h) * T, :]

    @pl.when(odd == 0)
    def _():
        half(0, keep)
        half(1, send)

    @pl.when(odd == 1)
    def _():
        half(1, keep)
        half(0, send)


def right_kernel(mine, other, tile, first, second, out, send_a, send_b, held, middle):
    row, c = lax.axis_index("row"), lax.axis_index("col")
    y, xh, core = row // (XH * CORE), (row // CORE) % XH, row % CORE
    odd = c % 2
    for source, k in ((mine, core), (other, 1 - core)):
        for i in range(Y):
            for e, x in enumerate((xh, 1 - xh)):
                at = 2 * (((y ^ i) * XH + x) * CORE + k)
                place(held, source, i * 4 + e * 2, at + odd, 8)
                place(held, source, i * 4 + e * 2 + 1, at + 1 - odd, 8)
    even = odd == 0
    before = jnp.where(even, second[...], first[...])
    after = jnp.where(even, first[...], second[...])
    whole = jnp.concatenate([before, tile[...], after], axis=1)
    for j in range(5):
        window = whole[:, j * B : (j + 3) * B]
        middle[:, j * B : (j + 1) * B] = product(window, wide(held, j), ((1,), (1,)))
    for j in range(3):
        window = middle[:, j * B : (j + 3) * B]
        out[:, j * B : (j + 1) * B] = product(window, wide(held, 5 + j), ((1,), (1,)))
    height = out.shape[0]

    @pl.when(core == 0)
    def _():
        send_a[...] = out[height - 2 * B :, :]
        send_b[...] = out[: 2 * B, :]

    @pl.when(core == 1)
    def _():
        send_a[...] = out[: 2 * B, :]
        send_b[...] = out[height - 2 * B :, :]


def gather_kernel(m0, m1, held):
    core, z = lax.axis_index("row") % 2, lax.axis_index("col") % Z
    sign = 1 - 2 * core
    for i, near in enumerate(NEAR):
        for j, far in enumerate(FAR):
            source, slot = (m0, j) if i == 0 else (m1, (i - 1) * 4 + j)
            place(held, source, slot, (z + sign * near + far + Z) % Z, 14)


def left_kernel(half, o0, o1, tile, first, second, noise, places, out, held, middle):
    row, col = lax.axis_index("row"), lax.axis_index("col")
    core, xl, z = row % 2, col // Z, col % Z
    sign = 1 - 2 * core
    start = pl.multiple_of(xl * Z * T, 8)
    for q in range(14):
        held[q, pl.ds(start, Z * T), :] = half[q]
    for i, near in enumerate(NEAR):
        for j, far in enumerate(FAR):
            source, slot = (o0, j) if i == 0 else (o1, (i - 1) * 4 + j)
            place(held, source, slot, (1 - xl) * Z + (z + sign * near + far + Z) % Z, 14)
    even = core == 0
    before = jnp.where(even, second[...], first[...])
    after = jnp.where(even, first[...], second[...])
    whole = jnp.concatenate([before, tile[...], after], axis=0)
    for i in range(8):
        window = whole[i * B : (i + 3) * B, :]
        middle[i * B : (i + 1) * B, :] = product(wide(held, i), window, ((1,), (0,)))
    across = jnp.concatenate([places[pl.ds(col * 3 + j, 1), :] for j in range(3)], axis=1)
    for i in range(6):
        rows = slice(i * B, (i + 1) * B)
        window = middle[i * B : (i + 3) * B, :]
        total = product(wide(held, 8 + i), window, ((1,), (0,)))
        down = jnp.transpose(jnp.broadcast_to(places[pl.ds(row * 6 + i, 1), :], (B, B)))
        distance = (jnp.concatenate([down] * 3, axis=1) - across) / 0.5
        out[rows, :] = total * jnp.exp(-distance * distance) + noise[rows, :]


def local(kernel, outs, scratch=(), flops=0, limit=None):
    vmem = pl.BlockSpec(memory_space=pltpu.VMEM)

    def call(*args):
        return pl.pallas_call(
            kernel,
            out_shape=[jax.ShapeDtypeStruct(o, jnp.float32) for o in outs],
            in_specs=[vmem] * len(args),
            out_specs=[vmem] * len(outs),
            scratch_shapes=[pltpu.VMEM(s, jnp.float32) for s in scratch],
            compiler_params=pltpu.CompilerParams(vmem_limit_bytes=limit),
            cost_estimate=pl.CostEstimate(flops=flops, bytes_accessed=1 << 20, transcendentals=0),
        )(*args)

    return call


def body(factors, covariance, noise, positions):
    height, width = covariance.shape
    even = lax.axis_index("col") % 2 == 0

    base, edge_a, edge_b = local(spread_kernel, [(14 * T, B), (T, B), (T, B)], limit=4 << 20)(factors)
    edge_a = swap_rows(edge_a, False)
    edge_b = swap_rows(edge_b, True)
    own, keep, send = local(halves_kernel, [(14 * T, B), (8 * T, B), (8 * T, B)], limit=4 << 20)(base, edge_a, edge_b)

    far = jnp.stack([shift_z(own, -d) for d in FAR])

    turned = turn(jnp.stack([keep, swap_cols(send, False)]))
    turned = jnp.concatenate([turned, flip_row(turned, CORE)])
    turned = jnp.concatenate([turned, flip_row(turned, XH * CORE)])
    mine = jnp.concatenate([turned, flip_row(turned, 2 * XH * CORE)])
    other = flip_row(mine, 1)

    near = jnp.concatenate([shift_near(far, -d) for d in NEAR[1:]])
    cross_far = flip_xl(far)
    cross_near = flip_xl(near)

    head, tail = covariance[:, : 2 * B], covariance[:, width - 2 * B :]
    first = swap_cols(jnp.where(even, tail, head), False)
    second = swap_cols(jnp.where(even, head, tail), True)
    edge = (2 * B, width)
    moved, send_a, send_b = local(
        right_kernel, [(height, width), edge, edge], [(8, 3 * B, B), (height, 5 * B)], 2000000000, 24 << 20
    )(mine, other, covariance, first, second)
    first = swap_rows(send_a, False)
    second = swap_rows(send_b, True)

    (half,) = local(gather_kernel, [(14, Z * T, B)], flops=1000000, limit=8 << 20)(far, near)
    (out,) = local(left_kernel, [(height, width)], [(14, 3 * B, B), (8 * B, width)], 2000000000, 28 << 20)(
        half, cross_far, cross_near, moved, first, second, noise, positions.reshape(-1, B)
    )
    return out


def solution(mesh):
    placed = (P(None, "row", "col"), P("row", "col"), P("row", "col"), P())
    return jax.shard_map(body, mesh=mesh, in_specs=placed, out_specs=P("row", "col"), check_vma=False)
```

```python
import jax
import jax.numpy as jnp
from jax import lax
from jax.experimental import pallas as pl
from jax.experimental.pallas import tpu as pltpu
from jax.sharding import PartitionSpec as P

B = 128
T = 12
XL, Z = 2, 16
Y, XH, CORE = 4, 2, 2
ROWS, COLS = Y * XH * CORE, XL * Z
BOTH = ("row", "col")
FAR = (-6, -2, 2, 6)
NEAR = (0, -1, 1, -2)


def move(x, target):
    pairs = []
    for r in range(ROWS):
        for c in range(COLS):
            to = target(r, c)
            if to is not None:
                pairs.append((r * COLS + c, to[0] * COLS + to[1]))
    return lax.ppermute(x, BOTH, pairs)


def odd_pair(i, count):
    j = i + 1 if i % 2 else i - 1
    return j if 0 <= j < count else None


def swap_rows(x, odd):
    def target(r, c):
        to = odd_pair(r, ROWS) if odd else r ^ 1
        return None if to is None else (to, c)

    return move(x, target)


def swap_cols(x, odd):
    def target(r, c):
        to = odd_pair(c, COLS) if odd else c ^ 1
        return None if to is None else (r, to)

    return move(x, target)


def shift_z(x, d):
    return move(x, lambda r, c: (r, c // Z * Z + (c % Z + d) % Z))


def shift_near(x, d):
    return move(x, lambda r, c: (r, c // Z * Z + (c % Z + (d if r % 2 == 0 else -d)) % Z))


def flip_row(x, bit):
    return move(x, lambda r, c: (r ^ bit, c))


def flip_xl(x):
    return move(x, lambda r, c: (r, (c + Z) % COLS))


def turn(x):
    def target(r, c):
        xl, z = divmod(c, Z)
        return (z % Y * XH + z // Y % XH) * CORE + z // (Y * XH), 2 * r + xl

    return move(x, target)


def split(x):
    hi = x.astype(jnp.bfloat16)
    return hi, (x - hi.astype(jnp.float32)).astype(jnp.bfloat16)


def product(a, b, contract):
    dims = (contract, ((), ()))
    ah, al = split(a)
    bh, bl = split(b)
    out = lax.dot_general(al, bh, dims, preferred_element_type=jnp.float32)
    out += lax.dot_general(ah, bl, dims, preferred_element_type=jnp.float32)
    return out + lax.dot_general(ah, bh, dims, preferred_element_type=jnp.float32)


def wide(ref, q):
    return jnp.concatenate([ref[q, k * B : (k + 1) * B, :] for k in range(3)], axis=1)


def place(held, piece, slot, at, count):
    start = pl.multiple_of(at * T, 4)
    for q in range(count):
        held[q, pl.ds(start, T), :] = piece[slot, q * T : (q + 1) * T, :]


def spread_kernel(factors, base, first, second):
    core = lax.axis_index("row") % 2
    base[0:T, :] = jnp.zeros((T, B), jnp.float32)
    base[7 * T : 8 * T, :] = jnp.zeros((T, B), jnp.float32)
    for f, at in ((0, 1), (1, 8)):
        for t in range(T):
            base[pl.ds(at * T + t, 6, stride=T), :] = factors[f, :, t * B : (t + 1) * B]
    top, bottom = base[T : 2 * T, :], base[6 * T : 7 * T, :]

    @pl.when(core == 0)
    def _():
        first[...] = bottom
        second[...] = top

    @pl.when(core == 1)
    def _():
        first[...] = top
        second[...] = bottom


def halves_kernel(base, first, second, own, keep, send):
    core, odd = lax.axis_index("row") % 2, lax.axis_index("col") // Z
    own[...] = base[...]

    @pl.when(core == 0)
    def _():
        own[0:T, :] = second[...]
        own[7 * T : 8 * T, :] = first[...]

    @pl.when(core == 1)
    def _():
        own[0:T, :] = first[...]
        own[7 * T : 8 * T, :] = second[...]

    def half(h, out):
        out[0 : 5 * T, :] = own[3 * h * T : (3 * h + 5) * T, :]
        out[5 * T : 8 * T, :] = own[(8 + 3 * h) * T : (11 + 3 * h) * T, :]

    @pl.when(odd == 0)
    def _():
        half(0, keep)
        half(1, send)

    @pl.when(odd == 1)
    def _():
        half(1, keep)
        half(0, send)


def right_kernel(mine, other, tile, first, second, out, send_a, send_b, held, middle):
    row, c = lax.axis_index("row"), lax.axis_index("col")
    y, xh, core = row // (XH * CORE), (row // CORE) % XH, row % CORE
    odd = c % 2
    for source, k in ((mine, core), (other, 1 - core)):
        for i in range(Y):
            for e, x in enumerate((xh, 1 - xh)):
                at = (y ^ i) + Y * x + Y * XH * k
                place(held, source, i * 4 + e * 2, at + Z * odd, 8)
                place(held, source, i * 4 + e * 2 + 1, at + Z * (1 - odd), 8)
    even = odd == 0
    before = jnp.where(even, second[...], first[...])
    after = jnp.where(even, first[...], second[...])
    whole = jnp.concatenate([before, tile[...], after], axis=1)
    for j in range(5):
        window = whole[:, j * B : (j + 3) * B]
        middle[:, j * B : (j + 1) * B] = product(window, wide(held, j), ((1,), (1,)))
    for j in range(3):
        window = middle[:, j * B : (j + 3) * B]
        out[:, j * B : (j + 1) * B] = product(window, wide(held, 5 + j), ((1,), (1,)))
    height = out.shape[0]

    @pl.when(core == 0)
    def _():
        send_a[...] = out[height - 2 * B :, :]
        send_b[...] = out[: 2 * B, :]

    @pl.when(core == 1)
    def _():
        send_a[...] = out[: 2 * B, :]
        send_b[...] = out[height - 2 * B :, :]


def gather_kernel(m0, m1, m2, held):
    core, z = lax.axis_index("row") % 2, lax.axis_index("col") % Z
    sign = 1 - 2 * core
    for i, near in enumerate(NEAR):
        for j, far in enumerate(FAR):
            source, slot = ((m0, j), (m1, j), (m1, 4 + j), (m2, j))[i]
            place(held, source, slot, (z + sign * near + far + Z) % Z, 14)


def left_kernel(half, o0, o1, o2, tile, first, second, noise, places, out, held, middle):
    row, col = lax.axis_index("row"), lax.axis_index("col")
    core, xl, z = row % 2, col // Z, col % Z
    sign = 1 - 2 * core
    start = pl.multiple_of(xl * Z * T, 8)
    for q in range(14):
        held[q, pl.ds(start, Z * T), :] = half[q]
    for i, near in enumerate(NEAR):
        for j, far in enumerate(FAR):
            source, slot = ((o0, j), (o1, j), (o1, 4 + j), (o2, j))[i]
            place(held, source, slot, (1 - xl) * Z + (z + sign * near + far + Z) % Z, 14)
    even = core == 0
    before = jnp.where(even, second[...], first[...])
    after = jnp.where(even, first[...], second[...])
    whole = jnp.concatenate([before, tile[...], after], axis=0)
    for i in range(8):
        window = whole[i * B : (i + 3) * B, :]
        middle[i * B : (i + 1) * B, :] = product(wide(held, i), window, ((1,), (0,)))
    across = jnp.concatenate([places[pl.ds(col * 3 + j, 1), :] for j in range(3)], axis=1)
    for i in range(6):
        rows = slice(i * B, (i + 1) * B)
        window = middle[i * B : (i + 3) * B, :]
        total = product(wide(held, 8 + i), window, ((1,), (0,)))
        down = jnp.transpose(jnp.broadcast_to(places[pl.ds(row * 6 + i, 1), :], (B, B)))
        distance = (jnp.concatenate([down] * 3, axis=1) - across) / 0.5
        out[rows, :] = total * jnp.exp(-distance * distance) + noise[rows, :]


def local(kernel, outs, scratch=(), flops=0, limit=None):
    vmem = pl.BlockSpec(memory_space=pltpu.VMEM)

    def call(*args):
        return pl.pallas_call(
            kernel,
            out_shape=[jax.ShapeDtypeStruct(o, jnp.float32) for o in outs],
            in_specs=[vmem] * len(args),
            out_specs=[vmem] * len(outs),
            scratch_shapes=[pltpu.VMEM(s, jnp.float32) for s in scratch],
            compiler_params=pltpu.CompilerParams(vmem_limit_bytes=limit),
            cost_estimate=pl.CostEstimate(flops=flops, bytes_accessed=1 << 20, transcendentals=0),
        )(*args)

    return call


def body(factors, covariance, noise, positions):
    height, width = covariance.shape
    even = lax.axis_index("col") % 2 == 0

    base, edge_a, edge_b = local(spread_kernel, [(14 * T, B), (T, B), (T, B)], limit=4 << 20)(factors)
    edge_a = swap_rows(edge_a, False)
    edge_b = swap_rows(edge_b, True)
    own, keep, send = local(halves_kernel, [(14 * T, B), (8 * T, B), (8 * T, B)], limit=4 << 20)(base, edge_a, edge_b)

    far = jnp.stack([shift_z(own, -d) for d in FAR])

    turned = turn(jnp.stack([keep, flip_xl(send)]))
    turned = jnp.concatenate([turned, flip_row(turned, CORE)])
    turned = jnp.concatenate([turned, flip_row(turned, XH * CORE)])
    mine = jnp.concatenate([turned, flip_row(turned, 2 * XH * CORE)])
    other = flip_row(mine, 1)

    near = [shift_near(far, -d) for d in NEAR[1:]]
    blocks = far, jnp.concatenate(near[:2]), near[2]
    cross = [flip_xl(x) for x in blocks]

    head, tail = covariance[:, : 2 * B], covariance[:, width - 2 * B :]
    first = swap_cols(jnp.where(even, tail, head), False)
    second = swap_cols(jnp.where(even, head, tail), True)
    edge = (2 * B, width)
    moved, send_a, send_b = local(
        right_kernel, [(height, width), edge, edge], [(8, 3 * B, B), (height, 5 * B)], 2000000000, 24 << 20
    )(mine, other, covariance, first, second)
    first = swap_rows(send_a, False)
    second = swap_rows(send_b, True)

    (half,) = local(gather_kernel, [(14, Z * T, B)], flops=1000000, limit=8 << 20)(*blocks)
    (out,) = local(left_kernel, [(height, width)], [(14, 3 * B, B), (8 * B, width)], 2000000000, 28 << 20)(
        half, *cross, moved, first, second, noise, positions.reshape(-1, B)
    )
    return out


def solution(mesh):
    placed = (P(None, "row", "col"), P("row", "col"), P("row", "col"), P())
    return jax.shard_map(body, mesh=mesh, in_specs=placed, out_specs=P("row", "col"), check_vma=False)
```

```python
import jax
import jax.numpy as jnp
from jax import lax
from jax.experimental import pallas as pl
from jax.experimental.pallas import tpu as pltpu
from jax.sharding import PartitionSpec as P

B = 128
T = 12
XL, Z = 2, 16
Y, XH, CORE = 4, 2, 2
ROWS, COLS = Y * XH * CORE, XL * Z
BOTH = ("row", "col")
FAR = (0, -4, 4, 8)
NEAR = (0, -1, 1, -2)


def move(x, target):
    pairs = []
    for r in range(ROWS):
        for c in range(COLS):
            to = target(r, c)
            if to is not None:
                pairs.append((r * COLS + c, to[0] * COLS + to[1]))
    return lax.ppermute(x, BOTH, pairs)


def odd_pair(i, count):
    j = i + 1 if i % 2 else i - 1
    return j if 0 <= j < count else None


def swap_rows(x, odd):
    def target(r, c):
        to = odd_pair(r, ROWS) if odd else r ^ 1
        return None if to is None else (to, c)

    return move(x, target)


def swap_cols(x, odd):
    def target(r, c):
        to = odd_pair(c, COLS) if odd else c ^ 1
        return None if to is None else (r, to)

    return move(x, target)


def shift_z(x, d):
    return move(x, lambda r, c: (r, c // Z * Z + (c % Z + d) % Z))


def shift_near(x, d):
    return move(x, lambda r, c: (r, c // Z * Z + (c % Z + (d if r % 2 == 0 else -d)) % Z))


def fold_y(x):
    return move(x, lambda r, c: (r ^ (Y - 1) * XH * CORE, c))


def flip_row(x, bit):
    return move(x, lambda r, c: (r ^ bit, c))


def flip_xl(x):
    return move(x, lambda r, c: (r, (c + Z) % COLS))


def turn(x):
    def target(r, c):
        xl, z = divmod(c, Z)
        return (z % Y * XH + z // Y % XH) * CORE + z // (Y * XH), 2 * r + xl

    return move(x, target)


def split(x):
    hi = x.astype(jnp.bfloat16)
    return hi, (x - hi.astype(jnp.float32)).astype(jnp.bfloat16)


def product(a, b, contract):
    dims = (contract, ((), ()))
    ah, al = split(a)
    bh, bl = split(b)
    out = lax.dot_general(al, bh, dims, preferred_element_type=jnp.float32)
    out += lax.dot_general(ah, bl, dims, preferred_element_type=jnp.float32)
    return out + lax.dot_general(ah, bh, dims, preferred_element_type=jnp.float32)


def wide(ref, q):
    return jnp.concatenate([ref[q, k * B : (k + 1) * B, :] for k in range(3)], axis=1)


def place(held, piece, slot, at, count):
    start = pl.multiple_of(at * T, 4)
    for q in range(count):
        held[q, pl.ds(start, T), :] = piece[slot, q * T : (q + 1) * T, :]


def spread_kernel(factors, base, first, second):
    core = lax.axis_index("row") % 2
    base[0:T, :] = jnp.zeros((T, B), jnp.float32)
    base[7 * T : 8 * T, :] = jnp.zeros((T, B), jnp.float32)
    for f, at in ((0, 1), (1, 8)):
        for t in range(T):
            base[pl.ds(at * T + t, 6, stride=T), :] = factors[f, :, t * B : (t + 1) * B]
    top, bottom = base[T : 2 * T, :], base[6 * T : 7 * T, :]

    @pl.when(core == 0)
    def _():
        first[...] = bottom
        second[...] = top

    @pl.when(core == 1)
    def _():
        first[...] = top
        second[...] = bottom


def halves_kernel(base, first, second, own, keep, send):
    core, odd = lax.axis_index("row") % 2, lax.axis_index("col") // Z
    own[...] = base[...]

    @pl.when(core == 0)
    def _():
        own[0:T, :] = second[...]
        own[7 * T : 8 * T, :] = first[...]

    @pl.when(core == 1)
    def _():
        own[0:T, :] = first[...]
        own[7 * T : 8 * T, :] = second[...]

    def half(h, out):
        out[0 : 5 * T, :] = own[3 * h * T : (3 * h + 5) * T, :]
        out[5 * T : 8 * T, :] = own[(8 + 3 * h) * T : (11 + 3 * h) * T, :]

    @pl.when(odd == 0)
    def _():
        half(0, keep)
        half(1, send)

    @pl.when(odd == 1)
    def _():
        half(1, keep)
        half(0, send)


def right_kernel(mine, other, tile, first, second, out, send_a, send_b, held, middle):
    row, c = lax.axis_index("row"), lax.axis_index("col")
    y, xh, core = row // (XH * CORE), (row // CORE) % XH, row % CORE
    odd = c % 2
    for source, k in ((mine, core), (other, 1 - core)):
        for i, bits in enumerate((0, 1, 3, 2)):
            for e, x in enumerate((xh, 1 - xh)):
                at = (y ^ bits) + Y * x + Y * XH * k
                place(held, source, i * 4 + e * 2, at + Z * odd, 8)
                place(held, source, i * 4 + e * 2 + 1, at + Z * (1 - odd), 8)
    even = odd == 0
    before = jnp.where(even, second[...], first[...])
    after = jnp.where(even, first[...], second[...])
    whole = jnp.concatenate([before, tile[...], after], axis=1)
    for j in range(5):
        window = whole[:, j * B : (j + 3) * B]
        middle[:, j * B : (j + 1) * B] = product(window, wide(held, j), ((1,), (1,)))
    for j in range(3):
        window = middle[:, j * B : (j + 3) * B]
        out[:, j * B : (j + 1) * B] = product(window, wide(held, 5 + j), ((1,), (1,)))
    height = out.shape[0]

    @pl.when(core == 0)
    def _():
        send_a[...] = out[height - 2 * B :, :]
        send_b[...] = out[: 2 * B, :]

    @pl.when(core == 1)
    def _():
        send_a[...] = out[: 2 * B, :]
        send_b[...] = out[height - 2 * B :, :]


def place_near(held, piece, slot, xl, near):
    core, z = lax.axis_index("row") % 2, lax.axis_index("col") % Z
    for j, far in enumerate(FAR):
        at = xl * Z + (z + (1 - 2 * core) * near + far + Z) % Z
        place(held, piece, slot + j, at, 14)


def gather_kernel(far, near, cross, held):
    xl = lax.axis_index("col") // Z
    place_near(held, far, 0, xl, NEAR[0])
    place_near(held, near, 0, xl, NEAR[1])
    place_near(held, near, 4, xl, NEAR[2])
    place_near(held, cross, 0, 1 - xl, NEAR[0])


def left_kernel(early, last, cross, tile, first, second, noise, places, out, held, middle):
    row, col = lax.axis_index("row"), lax.axis_index("col")
    core, xl = row % 2, col // Z
    held[...] = early[...]
    place_near(held, last, 0, xl, NEAR[3])
    place_near(held, last, 4, 1 - xl, NEAR[3])
    place_near(held, cross, 0, 1 - xl, NEAR[1])
    place_near(held, cross, 4, 1 - xl, NEAR[2])
    even = core == 0
    before = jnp.where(even, second[...], first[...])
    after = jnp.where(even, first[...], second[...])
    whole = jnp.concatenate([before, tile[...], after], axis=0)
    for i in range(8):
        window = whole[i * B : (i + 3) * B, :]
        middle[i * B : (i + 1) * B, :] = product(wide(held, i), window, ((1,), (0,)))
    across = jnp.concatenate([places[pl.ds(col * 3 + j, 1), :] for j in range(3)], axis=1)
    for i in range(6):
        rows = slice(i * B, (i + 1) * B)
        window = middle[i * B : (i + 3) * B, :]
        total = product(wide(held, 8 + i), window, ((1,), (0,)))
        down = jnp.transpose(jnp.broadcast_to(places[pl.ds(row * 6 + i, 1), :], (B, B)))
        distance = (jnp.concatenate([down] * 3, axis=1) - across) / 0.5
        out[rows, :] = total * jnp.exp(-distance * distance) + noise[rows, :]


def local(kernel, outs, scratch=(), flops=0, limit=None):
    vmem = pl.BlockSpec(memory_space=pltpu.VMEM)

    def call(*args):
        return pl.pallas_call(
            kernel,
            out_shape=[jax.ShapeDtypeStruct(o, jnp.float32) for o in outs],
            in_specs=[vmem] * len(args),
            out_specs=[vmem] * len(outs),
            scratch_shapes=[pltpu.VMEM(s, jnp.float32) for s in scratch],
            compiler_params=pltpu.CompilerParams(vmem_limit_bytes=limit),
            cost_estimate=pl.CostEstimate(flops=flops, bytes_accessed=1 << 20, transcendentals=0),
        )(*args)

    return call


def body(factors, covariance, noise, positions):
    height, width = covariance.shape
    even = lax.axis_index("col") % 2 == 0

    base, edge_a, edge_b = local(spread_kernel, [(14 * T, B), (T, B), (T, B)], limit=4 << 20)(factors)
    edge_a = swap_rows(edge_a, False)
    edge_b = swap_rows(edge_b, True)
    own, keep, send = local(halves_kernel, [(14 * T, B), (8 * T, B), (8 * T, B)], limit=4 << 20)(base, edge_a, edge_b)

    far = jnp.stack([own] + [shift_z(own, -d) for d in FAR[1:]])

    turned = turn(jnp.stack([keep, flip_xl(send)]))
    turned = jnp.concatenate([turned, flip_row(turned, CORE)])
    turned = jnp.concatenate([turned, flip_row(turned, XH * CORE)])
    mine = jnp.concatenate([turned, fold_y(turned)])
    other = flip_row(mine, 1)

    near = jnp.concatenate([shift_near(far, -NEAR[1]), shift_near(far, -NEAR[2])])
    cross = flip_xl(far)
    last = shift_near(jnp.concatenate([far, cross]), -NEAR[3])
    cross_near = flip_xl(near)

    head, tail = covariance[:, : 2 * B], covariance[:, width - 2 * B :]
    first = swap_cols(jnp.where(even, tail, head), False)
    second = swap_cols(jnp.where(even, head, tail), True)
    edge = (2 * B, width)
    moved, send_a, send_b = local(
        right_kernel, [(height, width), edge, edge], [(8, 3 * B, B), (height, 5 * B)], 2000000000, 24 << 20
    )(mine, other, covariance, first, second)
    first = swap_rows(send_a, False)
    second = swap_rows(send_b, True)

    (early,) = local(gather_kernel, [(14, 3 * B, B)], flops=1000000, limit=12 << 20)(far, near, cross)
    (out,) = local(left_kernel, [(height, width)], [(14, 3 * B, B), (8 * B, width)], 2000000000, 28 << 20)(
        early, last, cross_near, moved, first, second, noise, positions.reshape(-1, B)
    )
    return out


def solution(mesh):
    placed = (P(None, "row", "col"), P("row", "col"), P("row", "col"), P())
    return jax.shard_map(body, mesh=mesh, in_specs=placed, out_specs=P("row", "col"), check_vma=False)
```

```python
import jax
import jax.numpy as jnp
from jax import lax
from jax.experimental import pallas as pl
from jax.experimental.pallas import tpu as pltpu
from jax.sharding import PartitionSpec as P

B = 128
T = 12
XL, Z = 2, 16
Y, XH, CORE = 4, 2, 2
ROWS, COLS = Y * XH * CORE, XL * Z
BOTH = ("row", "col")
FAR = (0, -4, 4, 8)
NEAR = (0, -1, 1, -2)


def move(x, target):
    pairs = []
    for r in range(ROWS):
        for c in range(COLS):
            to = target(r, c)
            if to is not None:
                pairs.append((r * COLS + c, to[0] * COLS + to[1]))
    return lax.ppermute(x, BOTH, pairs)


def odd_pair(i, count):
    j = i + 1 if i % 2 else i - 1
    return j if 0 <= j < count else None


def swap_rows(x, odd):
    def target(r, c):
        to = odd_pair(r, ROWS) if odd else r ^ 1
        return None if to is None else (to, c)

    return move(x, target)


def swap_cols(x, odd):
    def target(r, c):
        to = odd_pair(c, COLS) if odd else c ^ 1
        return None if to is None else (r, to)

    return move(x, target)


def shift_z(x, d):
    return move(x, lambda r, c: (r, c // Z * Z + (c % Z + d) % Z))


def shift_near(x, d):
    return move(x, lambda r, c: (r, c // Z * Z + (c % Z + (d if r % 2 == 0 else -d)) % Z))


def fold_y(x):
    return move(x, lambda r, c: (r ^ (Y - 1) * XH * CORE, c))


def flip_row(x, bit):
    return move(x, lambda r, c: (r ^ bit, c))


def flip_xl(x):
    return move(x, lambda r, c: (r, (c + Z) % COLS))


def turn(x):
    def target(r, c):
        xl, z = divmod(c, Z)
        return (z % Y * XH + z // Y % XH) * CORE + z // (Y * XH), 2 * r + xl

    return move(x, target)


def split(x):
    hi = x.astype(jnp.bfloat16)
    return hi, (x - hi.astype(jnp.float32)).astype(jnp.bfloat16)


def product(a, b, contract):
    dims = (contract, ((), ()))
    ah, al = split(a)
    bh, bl = split(b)
    out = lax.dot_general(al, bh, dims, preferred_element_type=jnp.float32)
    out += lax.dot_general(ah, bl, dims, preferred_element_type=jnp.float32)
    return out + lax.dot_general(ah, bh, dims, preferred_element_type=jnp.float32)


def wide(ref, q):
    return jnp.concatenate([ref[q, k * B : (k + 1) * B, :] for k in range(3)], axis=1)


def place(held, piece, slot, at, count):
    start = pl.multiple_of(at * T, 4)
    for q in range(count):
        held[q, pl.ds(start, T), :] = piece[slot, q * T : (q + 1) * T, :]


def spread_kernel(factors, base, first, second):
    core = lax.axis_index("row") % 2
    base[0:T, :] = jnp.zeros((T, B), jnp.float32)
    base[7 * T : 8 * T, :] = jnp.zeros((T, B), jnp.float32)
    for f, at in ((0, 1), (1, 8)):
        for t in range(T):
            base[pl.ds(at * T + t, 6, stride=T), :] = factors[f, :, t * B : (t + 1) * B]
    top, bottom = base[T : 2 * T, :], base[6 * T : 7 * T, :]

    @pl.when(core == 0)
    def _():
        first[...] = bottom
        second[...] = top

    @pl.when(core == 1)
    def _():
        first[...] = top
        second[...] = bottom


def halves_kernel(base, first, second, own, keep, send):
    core, odd = lax.axis_index("row") % 2, lax.axis_index("col") // Z
    own[...] = base[...]

    @pl.when(core == 0)
    def _():
        own[0:T, :] = second[...]
        own[7 * T : 8 * T, :] = first[...]

    @pl.when(core == 1)
    def _():
        own[0:T, :] = first[...]
        own[7 * T : 8 * T, :] = second[...]

    def half(h, out):
        out[0 : 5 * T, :] = own[3 * h * T : (3 * h + 5) * T, :]
        out[5 * T : 8 * T, :] = own[(8 + 3 * h) * T : (11 + 3 * h) * T, :]

    @pl.when(odd == 0)
    def _():
        half(0, keep)
        half(1, send)

    @pl.when(odd == 1)
    def _():
        half(1, keep)
        half(0, send)


def extend_kernel(tile, first, second, out, send_a, send_b):
    core, odd = lax.axis_index("row") % 2, lax.axis_index("col") % 2
    height, width = tile.shape
    out[2 * B : 2 * B + height, :] = tile[...]

    @pl.when(core == 0)
    def _():
        out[: 2 * B, :] = second[...]
        out[2 * B + height :, :] = first[...]

    @pl.when(core == 1)
    def _():
        out[: 2 * B, :] = first[...]
        out[2 * B + height :, :] = second[...]

    @pl.when(odd == 0)
    def _():
        send_a[...] = out[:, width - 2 * B :]
        send_b[...] = out[:, : 2 * B]

    @pl.when(odd == 1)
    def _():
        send_a[...] = out[:, : 2 * B]
        send_b[...] = out[:, width - 2 * B :]


def right_kernel(mine, other, tile, first, second, out, held, middle):
    row, c = lax.axis_index("row"), lax.axis_index("col")
    y, xh, core = row // (XH * CORE), (row // CORE) % XH, row % CORE
    odd = c % 2
    for source, k in ((mine, core), (other, 1 - core)):
        for i, bits in enumerate((0, 1, 3, 2)):
            for e, x in enumerate((xh, 1 - xh)):
                at = (y ^ bits) + Y * x + Y * XH * k
                place(held, source, i * 4 + e * 2, at + Z * odd, 8)
                place(held, source, i * 4 + e * 2 + 1, at + Z * (1 - odd), 8)
    even = odd == 0
    half = out.shape[0] // 2
    for part in range(2):
        rows = slice(part * half, (part + 1) * half)
        before = jnp.where(even, second[rows, :], first[rows, :])
        after = jnp.where(even, first[rows, :], second[rows, :])
        whole = jnp.concatenate([before, tile[rows, :], after], axis=1)
        for j in range(5):
            window = whole[:, j * B : (j + 3) * B]
            middle[:, j * B : (j + 1) * B] = product(window, wide(held, j), ((1,), (1,)))
        for j in range(3):
            window = middle[:, j * B : (j + 3) * B]
            out[rows, j * B : (j + 1) * B] = product(window, wide(held, 5 + j), ((1,), (1,)))


def place_near(held, piece, slot, xl, near):
    core, z = lax.axis_index("row") % 2, lax.axis_index("col") % Z
    for j, far in enumerate(FAR):
        at = xl * Z + (z + (1 - 2 * core) * near + far + Z) % Z
        place(held, piece, slot + j, at, 14)


def gather_kernel(far, near, last, cross, held):
    xl = lax.axis_index("col") // Z
    place_near(held, far, 0, xl, NEAR[0])
    place_near(held, near, 0, xl, NEAR[1])
    place_near(held, near, 4, xl, NEAR[2])
    place_near(held, last, 0, xl, NEAR[3])
    place_near(held, cross, 0, 1 - xl, NEAR[0])


def left_kernel(early, cross, last, whole, noise, places, out, held, middle):
    row, col = lax.axis_index("row"), lax.axis_index("col")
    xl = col // Z
    held[...] = early[...]
    place_near(held, cross, 0, 1 - xl, NEAR[1])
    place_near(held, cross, 4, 1 - xl, NEAR[2])
    place_near(held, last, 0, 1 - xl, NEAR[3])
    for i in range(8):
        window = whole[i * B : (i + 3) * B, :]
        middle[i * B : (i + 1) * B, :] = product(wide(held, i), window, ((1,), (0,)))
    across = jnp.concatenate([places[pl.ds(col * 3 + j, 1), :] for j in range(3)], axis=1)
    for i in range(6):
        rows = slice(i * B, (i + 1) * B)
        window = middle[i * B : (i + 3) * B, :]
        total = product(wide(held, 8 + i), window, ((1,), (0,)))
        down = jnp.transpose(jnp.broadcast_to(places[pl.ds(row * 6 + i, 1), :], (B, B)))
        distance = (jnp.concatenate([down] * 3, axis=1) - across) / 0.5
        out[rows, :] = total * jnp.exp(-distance * distance) + noise[rows, :]


def local(kernel, outs, scratch=(), flops=0, limit=None):
    vmem = pl.BlockSpec(memory_space=pltpu.VMEM)

    def call(*args):
        return pl.pallas_call(
            kernel,
            out_shape=[jax.ShapeDtypeStruct(o, jnp.float32) for o in outs],
            in_specs=[vmem] * len(args),
            out_specs=[vmem] * len(outs),
            scratch_shapes=[pltpu.VMEM(s, jnp.float32) for s in scratch],
            compiler_params=pltpu.CompilerParams(vmem_limit_bytes=limit),
            cost_estimate=pl.CostEstimate(flops=flops, bytes_accessed=1 << 20, transcendentals=0),
        )(*args)

    return call


def body(factors, covariance, noise, positions):
    height, width = covariance.shape
    above = lax.axis_index("row") % 2 == 0

    head, tail = covariance[: 2 * B], covariance[height - 2 * B :]
    first = swap_rows(jnp.where(above, tail, head), False)
    second = swap_rows(jnp.where(above, head, tail), True)
    tall, sides = (height + 4 * B, width), (height + 4 * B, 2 * B)
    tile, send_a, send_b = local(extend_kernel, [tall, sides, sides], limit=12 << 20)(covariance, first, second)
    first = swap_cols(send_a, False)
    second = swap_cols(send_b, True)

    base, edge_a, edge_b = local(spread_kernel, [(14 * T, B), (T, B), (T, B)], limit=4 << 20)(factors)
    edge_a = swap_rows(edge_a, False)
    edge_b = swap_rows(edge_b, True)
    own, keep, send = local(halves_kernel, [(14 * T, B), (8 * T, B), (8 * T, B)], limit=4 << 20)(base, edge_a, edge_b)

    far = jnp.stack([own] + [shift_z(own, -d) for d in FAR[1:]])

    turned = turn(jnp.stack([keep, flip_xl(send)]))
    turned = jnp.concatenate([turned, flip_row(turned, CORE)])
    turned = jnp.concatenate([turned, flip_row(turned, XH * CORE)])
    mine = jnp.concatenate([turned, fold_y(turned)])
    other = flip_row(mine, 1)

    near = [shift_near(far, -NEAR[1]), shift_near(far, -NEAR[2])]
    last = shift_near(near[0], -NEAR[1])
    near = jnp.concatenate(near)
    cross, cross_near, cross_last = (flip_xl(x) for x in (far, near, last))

    (moved,) = local(right_kernel, [tall], [(8, 3 * B, B), (tall[0] // 2, 5 * B)], 3000000000, 28 << 20)(
        mine, other, tile, first, second
    )
    (early,) = local(gather_kernel, [(14, 3 * B, B)], flops=1000000, limit=12 << 20)(far, near, last, cross)
    (out,) = local(left_kernel, [(height, width)], [(14, 3 * B, B), (8 * B, width)], 2000000000, 28 << 20)(
        early, cross_near, cross_last, moved, noise, positions.reshape(-1, B)
    )
    return out


def solution(mesh):
    placed = (P(None, "row", "col"), P("row", "col"), P("row", "col"), P())
    return jax.shard_map(body, mesh=mesh, in_specs=placed, out_specs=P("row", "col"), check_vma=False)
```

```python
import jax
import jax.numpy as jnp
from jax import lax
from jax.experimental import pallas as pl
from jax.experimental.pallas import tpu as pltpu
from jax.sharding import PartitionSpec as P

B = 128
T = 12
XL, Z = 2, 16
Y, XH, CORE = 4, 2, 2
ROWS, COLS = Y * XH * CORE, XL * Z
BOTH = ("row", "col")
FAR = (0, -4, 4, 8)
NEAR = (0, -1, 1, -2)


def move(x, target):
    pairs = []
    for r in range(ROWS):
        for c in range(COLS):
            to = target(r, c)
            if to is not None:
                pairs.append((r * COLS + c, to[0] * COLS + to[1]))
    return lax.ppermute(x, BOTH, pairs)


def odd_pair(i, count):
    j = i + 1 if i % 2 else i - 1
    return j if 0 <= j < count else None


def swap_rows(x, odd):
    def target(r, c):
        to = odd_pair(r, ROWS) if odd else r ^ 1
        return None if to is None else (to, c)

    return move(x, target)


def swap_cols(x, odd):
    def target(r, c):
        to = odd_pair(c, COLS) if odd else c ^ 1
        return None if to is None else (r, to)

    return move(x, target)


def shift_z(x, d):
    return move(x, lambda r, c: (r, c // Z * Z + (c % Z + d) % Z))


def shift_near(x, d):
    return move(x, lambda r, c: (r, c // Z * Z + (c % Z + (d if r % 2 == 0 else -d)) % Z))


def fold_y(x):
    return move(x, lambda r, c: (r ^ (Y - 1) * XH * CORE, c))


def flip_row(x, bit):
    return move(x, lambda r, c: (r ^ bit, c))


def flip_xl(x):
    return move(x, lambda r, c: (r, (c + Z) % COLS))


def turn(x):
    def target(r, c):
        xl, z = divmod(c, Z)
        return (z % Y * XH + z // Y % XH) * CORE + z // (Y * XH), 2 * r + xl

    return move(x, target)


def split(x):
    hi = x.astype(jnp.bfloat16)
    return hi, (x - hi.astype(jnp.float32)).astype(jnp.bfloat16)


def product(a, b, contract):
    dims = (contract, ((), ()))
    ah, al = split(a)
    bh, bl = split(b)
    out = lax.dot_general(al, bh, dims, preferred_element_type=jnp.float32)
    out += lax.dot_general(ah, bl, dims, preferred_element_type=jnp.float32)
    return out + lax.dot_general(ah, bh, dims, preferred_element_type=jnp.float32)


def wide(ref, q):
    return jnp.concatenate([ref[q, k * B : (k + 1) * B, :] for k in range(3)], axis=1)


def place(held, piece, slot, at, count):
    start = pl.multiple_of(at * T, 4)
    for q in range(count):
        held[q, pl.ds(start, T), :] = piece[slot, q * T : (q + 1) * T, :]


def spread_kernel(factors, base, first, second):
    core = lax.axis_index("row") % 2
    base[0:T, :] = jnp.zeros((T, B), jnp.float32)
    base[7 * T : 8 * T, :] = jnp.zeros((T, B), jnp.float32)
    for f, at in ((0, 1), (1, 8)):
        for t in range(T):
            base[pl.ds(at * T + t, 6, stride=T), :] = factors[f, :, t * B : (t + 1) * B]
    top, bottom = base[T : 2 * T, :], base[6 * T : 7 * T, :]

    @pl.when(core == 0)
    def _():
        first[...] = bottom
        second[...] = top

    @pl.when(core == 1)
    def _():
        first[...] = top
        second[...] = bottom


def halves_kernel(base, first, second, own, keep, send):
    core, odd = lax.axis_index("row") % 2, lax.axis_index("col") // Z
    own[...] = base[...]

    @pl.when(core == 0)
    def _():
        own[0:T, :] = second[...]
        own[7 * T : 8 * T, :] = first[...]

    @pl.when(core == 1)
    def _():
        own[0:T, :] = first[...]
        own[7 * T : 8 * T, :] = second[...]

    def half(h, out):
        out[0 : 5 * T, :] = own[3 * h * T : (3 * h + 5) * T, :]
        out[5 * T : 8 * T, :] = own[(8 + 3 * h) * T : (11 + 3 * h) * T, :]

    @pl.when(odd == 0)
    def _():
        half(0, keep)
        half(1, send)

    @pl.when(odd == 1)
    def _():
        half(1, keep)
        half(0, send)


def edges_kernel(first, second, out, send_a, send_b):
    core, odd = lax.axis_index("row") % 2, lax.axis_index("col") % 2
    width = out.shape[1]

    @pl.when(core == 0)
    def _():
        out[: 2 * B, :] = second[...]
        out[2 * B :, :] = first[...]

    @pl.when(core == 1)
    def _():
        out[: 2 * B, :] = first[...]
        out[2 * B :, :] = second[...]

    @pl.when(odd == 0)
    def _():
        send_a[...] = out[:, width - 2 * B :]
        send_b[...] = out[:, : 2 * B]

    @pl.when(odd == 1)
    def _():
        send_a[...] = out[:, : 2 * B]
        send_b[...] = out[:, width - 2 * B :]


def right_kernel(mine, other, tile, first, second, edges, edge_first, edge_second, out, held, middle):
    row, c = lax.axis_index("row"), lax.axis_index("col")
    y, xh, core = row // (XH * CORE), (row // CORE) % XH, row % CORE
    odd = c % 2
    for source, k in ((mine, core), (other, 1 - core)):
        for i, bits in enumerate((0, 1, 3, 2)):
            for e, x in enumerate((xh, 1 - xh)):
                at = (y ^ bits) + Y * x + Y * XH * k
                place(held, source, i * 4 + e * 2, at + Z * odd, 8)
                place(held, source, i * 4 + e * 2 + 1, at + Z * (1 - odd), 8)
    even = odd == 0
    height = tile.shape[0]
    half = height // 2
    parts = [(tile, first, second, i * half, half) for i in range(2)] + [(edges, edge_first, edge_second, 0, 4 * B)]
    for inner, a, b, start, count in parts:
        rows = slice(start, start + count)
        before = jnp.where(even, b[rows, :], a[rows, :])
        after = jnp.where(even, a[rows, :], b[rows, :])
        whole = jnp.concatenate([before, inner[rows, :], after], axis=1)
        for j in range(5):
            window = whole[:, j * B : (j + 3) * B]
            middle[:count, j * B : (j + 1) * B] = product(window, wide(held, j), ((1,), (1,)))
        for j in range(3):
            columns = slice(j * B, (j + 1) * B)
            total = product(middle[:count, j * B : (j + 3) * B], wide(held, 5 + j), ((1,), (1,)))
            if inner is tile:
                out[2 * B + start : 2 * B + start + count, columns] = total
            else:
                out[: 2 * B, columns] = total[: 2 * B]
                out[2 * B + height :, columns] = total[2 * B :]


def place_near(held, piece, slot, xl, near):
    core, z = lax.axis_index("row") % 2, lax.axis_index("col") % Z
    for j, far in enumerate(FAR):
        at = xl * Z + (z + (1 - 2 * core) * near + far + Z) % Z
        place(held, piece, slot + j, at, 14)


def gather_kernel(far, near, last, cross, held):
    xl = lax.axis_index("col") // Z
    place_near(held, far, 0, xl, NEAR[0])
    place_near(held, near, 0, xl, NEAR[1])
    place_near(held, near, 4, xl, NEAR[2])
    place_near(held, last, 0, xl, NEAR[3])
    place_near(held, cross, 0, 1 - xl, NEAR[0])


def left_kernel(early, cross, last, whole, noise, places, out, held, middle):
    row, col = lax.axis_index("row"), lax.axis_index("col")
    xl = col // Z
    held[...] = early[...]
    place_near(held, cross, 0, 1 - xl, NEAR[1])
    place_near(held, cross, 4, 1 - xl, NEAR[2])
    place_near(held, last, 0, 1 - xl, NEAR[3])
    for i in range(8):
        window = whole[i * B : (i + 3) * B, :]
        middle[i * B : (i + 1) * B, :] = product(wide(held, i), window, ((1,), (0,)))
    across = jnp.concatenate([places[pl.ds(col * 3 + j, 1), :] for j in range(3)], axis=1)
    for i in range(6):
        rows = slice(i * B, (i + 1) * B)
        window = middle[i * B : (i + 3) * B, :]
        total = product(wide(held, 8 + i), window, ((1,), (0,)))
        down = jnp.transpose(jnp.broadcast_to(places[pl.ds(row * 6 + i, 1), :], (B, B)))
        distance = (jnp.concatenate([down] * 3, axis=1) - across) / 0.5
        out[rows, :] = total * jnp.exp(-distance * distance) + noise[rows, :]


def local(kernel, outs, scratch=(), flops=0, limit=None):
    vmem = pl.BlockSpec(memory_space=pltpu.VMEM)

    def call(*args):
        return pl.pallas_call(
            kernel,
            out_shape=[jax.ShapeDtypeStruct(o, jnp.float32) for o in outs],
            in_specs=[vmem] * len(args),
            out_specs=[vmem] * len(outs),
            scratch_shapes=[pltpu.VMEM(s, jnp.float32) for s in scratch],
            compiler_params=pltpu.CompilerParams(vmem_limit_bytes=limit),
            cost_estimate=pl.CostEstimate(flops=flops, bytes_accessed=1 << 20, transcendentals=0),
        )(*args)

    return call


def body(factors, covariance, noise, positions):
    height, width = covariance.shape
    above, even = lax.axis_index("row") % 2 == 0, lax.axis_index("col") % 2 == 0

    head, tail = covariance[: 2 * B], covariance[height - 2 * B :]
    first = swap_rows(jnp.where(above, tail, head), False)
    second = swap_rows(jnp.where(above, head, tail), True)
    sides = (4 * B, 2 * B)
    edges, send_a, send_b = local(edges_kernel, [(4 * B, width), sides, sides], limit=4 << 20)(first, second)
    edge_first = swap_cols(send_a, False)
    edge_second = swap_cols(send_b, True)
    head, tail = covariance[:, : 2 * B], covariance[:, width - 2 * B :]
    first = swap_cols(jnp.where(even, tail, head), False)
    second = swap_cols(jnp.where(even, head, tail), True)

    base, edge_a, edge_b = local(spread_kernel, [(14 * T, B), (T, B), (T, B)], limit=4 << 20)(factors)
    edge_a = swap_rows(edge_a, False)
    edge_b = swap_rows(edge_b, True)
    own, keep, send = local(halves_kernel, [(14 * T, B), (8 * T, B), (8 * T, B)], limit=4 << 20)(base, edge_a, edge_b)

    far = jnp.stack([own] + [shift_z(own, -d) for d in FAR[1:]])

    turned = turn(jnp.stack([keep, flip_xl(send)]))
    turned = jnp.concatenate([turned, flip_row(turned, CORE)])
    turned = jnp.concatenate([turned, flip_row(turned, XH * CORE)])
    mine = jnp.concatenate([turned, fold_y(turned)])
    other = flip_row(mine, 1)

    near = [shift_near(far, -NEAR[1]), shift_near(far, -NEAR[2])]
    last = shift_near(near[0], -NEAR[1])
    near = jnp.concatenate(near)
    cross, cross_near, cross_last = (flip_xl(x) for x in (far, near, last))

    tall = (height + 4 * B, width)
    (moved,) = local(right_kernel, [tall], [(8, 3 * B, B), (4 * B, 5 * B)], 3000000000, 28 << 20)(
        mine, other, covariance, first, second, edges, edge_first, edge_second
    )
    (early,) = local(gather_kernel, [(14, 3 * B, B)], flops=1000000, limit=12 << 20)(far, near, last, cross)
    (out,) = local(left_kernel, [(height, width)], [(14, 3 * B, B), (8 * B, width)], 2000000000, 28 << 20)(
        early, cross_near, cross_last, moved, noise, positions.reshape(-1, B)
    )
    return out


def solution(mesh):
    placed = (P(None, "row", "col"), P("row", "col"), P("row", "col"), P())
    return jax.shard_map(body, mesh=mesh, in_specs=placed, out_specs=P("row", "col"), check_vma=False)
```

```python
import jax
import jax.numpy as jnp
from jax import lax
from jax.experimental import pallas as pl
from jax.experimental.pallas import tpu as pltpu
from jax.sharding import PartitionSpec as P

B = 128
T = 12
XL, Z = 2, 16
Y, XH, CORE = 4, 2, 2
ROWS, COLS = Y * XH * CORE, XL * Z
BOTH = ("row", "col")
FAR = (0, -4, 4, 8)
NEAR = (0, -1, 1, -2)


def move(x, target):
    pairs = []
    for r in range(ROWS):
        for c in range(COLS):
            to = target(r, c)
            if to is not None:
                pairs.append((r * COLS + c, to[0] * COLS + to[1]))
    return lax.ppermute(x, BOTH, pairs)


def odd_pair(i, count):
    j = i + 1 if i % 2 else i - 1
    return j if 0 <= j < count else None


def swap_rows(x, odd):
    def target(r, c):
        to = odd_pair(r, ROWS) if odd else r ^ 1
        return None if to is None else (to, c)

    return move(x, target)


def swap_cols(x, odd):
    def target(r, c):
        to = odd_pair(c, COLS) if odd else c ^ 1
        return None if to is None else (r, to)

    return move(x, target)


def shift_z(x, d):
    return move(x, lambda r, c: (r, c // Z * Z + (c % Z + d) % Z))


def shift_near(x, d):
    return move(x, lambda r, c: (r, c // Z * Z + (c % Z + (d if r % 2 == 0 else -d)) % Z))


def fold_y(x):
    return move(x, lambda r, c: (r ^ (Y - 1) * XH * CORE, c))


def flip_row(x, bit):
    return move(x, lambda r, c: (r ^ bit, c))


def flip_xl(x):
    return move(x, lambda r, c: (r, (c + Z) % COLS))


def turn(x):
    def target(r, c):
        xl, z = divmod(c, Z)
        return (z % Y * XH + z // Y % XH) * CORE + z // (Y * XH), 2 * r + xl

    return move(x, target)


def split(x):
    hi = x.astype(jnp.bfloat16)
    return hi, (x - hi.astype(jnp.float32)).astype(jnp.bfloat16)


def product(a, b, contract):
    dims = (contract, ((), ()))
    (ah, al), (bh, bl) = a, b
    out = lax.dot_general(al, bh, dims, preferred_element_type=jnp.float32)
    out += lax.dot_general(ah, bl, dims, preferred_element_type=jnp.float32)
    return out + lax.dot_general(ah, bh, dims, preferred_element_type=jnp.float32)


def wide(ref, q):
    return jnp.concatenate([ref[q, k * B : (k + 1) * B, :] for k in range(3)], axis=1)


def band(ref, q, count):
    if count == 1:
        return split(wide(ref, q))
    zero = jnp.zeros((B, B), jnp.float32)
    upper = jnp.concatenate([wide(ref, q), zero], axis=1)
    lower = jnp.concatenate([zero, wide(ref, q + 1)], axis=1)
    return split(jnp.concatenate([upper, lower], axis=0))


def place(held, piece, slot, at, count):
    start = pl.multiple_of(at * T, 4)
    for q in range(count):
        held[q, pl.ds(start, T), :] = piece[slot, q * T : (q + 1) * T, :]


def spread_kernel(factors, base, first, second):
    core = lax.axis_index("row") % 2
    base[0:T, :] = jnp.zeros((T, B), jnp.float32)
    base[7 * T : 8 * T, :] = jnp.zeros((T, B), jnp.float32)
    for f, at in ((0, 1), (1, 8)):
        for t in range(T):
            base[pl.ds(at * T + t, 6, stride=T), :] = factors[f, :, t * B : (t + 1) * B]
    top, bottom = base[T : 2 * T, :], base[6 * T : 7 * T, :]

    @pl.when(core == 0)
    def _():
        first[...] = bottom
        second[...] = top

    @pl.when(core == 1)
    def _():
        first[...] = top
        second[...] = bottom


def halves_kernel(base, first, second, own, keep, send):
    core, odd = lax.axis_index("row") % 2, lax.axis_index("col") // Z
    own[...] = base[...]

    @pl.when(core == 0)
    def _():
        own[0:T, :] = second[...]
        own[7 * T : 8 * T, :] = first[...]

    @pl.when(core == 1)
    def _():
        own[0:T, :] = first[...]
        own[7 * T : 8 * T, :] = second[...]

    def half(h, out):
        out[0 : 5 * T, :] = own[3 * h * T : (3 * h + 5) * T, :]
        out[5 * T : 8 * T, :] = own[(8 + 3 * h) * T : (11 + 3 * h) * T, :]

    @pl.when(odd == 0)
    def _():
        half(0, keep)
        half(1, send)

    @pl.when(odd == 1)
    def _():
        half(1, keep)
        half(0, send)


def edges_kernel(tile, first, second, send_a, send_b):
    core, even = lax.axis_index("row") % 2, lax.axis_index("col") % 2 == 0
    height = tile.shape[0]

    def rows(start, out):
        part = slice(start, start + 2 * B)
        before = jnp.where(even, second[part, :], first[part, :])
        after = jnp.where(even, first[part, :], second[part, :])
        out[...] = jnp.concatenate([before, tile[part, :], after], axis=1)

    @pl.when(core == 0)
    def _():
        rows(height - 2 * B, send_a)
        rows(0, send_b)

    @pl.when(core == 1)
    def _():
        rows(0, send_a)
        rows(height - 2 * B, send_b)


def right_kernel(mine, other, tile, first, second, edge_a, edge_b, out, held, high, low):
    row, c = lax.axis_index("row"), lax.axis_index("col")
    y, xh, core = row // (XH * CORE), (row // CORE) % XH, row % CORE
    odd = c % 2
    for source, k in ((mine, core), (other, 1 - core)):
        for i, bits in enumerate((0, 1, 3, 2)):
            for e, x in enumerate((xh, 1 - xh)):
                at = (y ^ bits) + Y * x + Y * XH * k
                place(held, source, i * 4 + e * 2, at + Z * odd, 8)
                place(held, source, i * 4 + e * 2 + 1, at + Z * (1 - odd), 8)
    even = odd == 0
    height = tile.shape[0]
    half = height // 2
    for part in range(3):
        if part < 2:
            rows = slice(part * half, (part + 1) * half)
            before = jnp.where(even, second[rows, :], first[rows, :])
            after = jnp.where(even, first[rows, :], second[rows, :])
            whole = jnp.concatenate([before, tile[rows, :], after], axis=1)
        else:
            above = jnp.where(core == 0, edge_b[...], edge_a[...])
            below = jnp.where(core == 0, edge_a[...], edge_b[...])
            whole = jnp.concatenate([above, below], axis=0)
        count = whole.shape[0]
        hi, lo = split(whole)
        for j, n in ((0, 2), (2, 2), (4, 1)):
            window = slice(j * B, (j + n + 2) * B)
            total = product((hi[:, window], lo[:, window]), band(held, j, n), ((1,), (1,)))
            columns = slice(j * B, (j + n) * B)
            high[:count, columns], low[:count, columns] = split(total)
        for j, n in ((0, 2), (2, 1)):
            window = slice(j * B, (j + n + 2) * B)
            total = product((high[:count, window], low[:count, window]), band(held, 5 + j, n), ((1,), (1,)))
            columns = slice(j * B, (j + n) * B)
            if part < 2:
                out[2 * B + part * half : 2 * B + (part + 1) * half, columns] = total
            else:
                out[: 2 * B, columns] = total[: 2 * B]
                out[2 * B + height :, columns] = total[2 * B :]


def place_near(held, piece, slot, xl, near):
    core, z = lax.axis_index("row") % 2, lax.axis_index("col") % Z
    for j, far in enumerate(FAR):
        at = xl * Z + (z + (1 - 2 * core) * near + far + Z) % Z
        place(held, piece, slot + j, at, 14)


def gather_kernel(far, near, last, cross, held):
    xl = lax.axis_index("col") // Z
    place_near(held, far, 0, xl, NEAR[0])
    place_near(held, near, 0, xl, NEAR[1])
    place_near(held, near, 4, xl, NEAR[2])
    place_near(held, last, 0, xl, NEAR[3])
    place_near(held, cross, 0, 1 - xl, NEAR[0])


def left_kernel(early, cross, last, whole, noise, places, out, held, high, low):
    row, col = lax.axis_index("row"), lax.axis_index("col")
    xl = col // Z
    held[...] = early[...]
    place_near(held, cross, 0, 1 - xl, NEAR[1])
    place_near(held, cross, 4, 1 - xl, NEAR[2])
    place_near(held, last, 0, 1 - xl, NEAR[3])
    whole_high, whole_low = split(whole[...])
    for i in range(0, 8, 2):
        window = slice(i * B, (i + 4) * B)
        total = product(band(held, i, 2), (whole_high[window, :], whole_low[window, :]), ((1,), (0,)))
        rows = slice(i * B, (i + 2) * B)
        high[rows, :], low[rows, :] = split(total)
    across = jnp.concatenate([places[pl.ds(col * 3 + j, 1), :] for j in range(3)], axis=1)
    for i in range(0, 6, 2):
        rows = slice(i * B, (i + 2) * B)
        window = slice(i * B, (i + 4) * B)
        total = product(band(held, 8 + i, 2), (high[window, :], low[window, :]), ((1,), (0,)))
        down = [jnp.transpose(jnp.broadcast_to(places[pl.ds(row * 6 + i + k, 1), :], (B, B))) for k in range(2)]
        down = jnp.concatenate([jnp.concatenate(down, axis=0)] * 3, axis=1)
        distance = (down - across) / 0.5
        out[rows, :] = total * jnp.exp(-distance * distance) + noise[rows, :]


def local(kernel, outs, scratch=(), flops=0, limit=None, halves=()):
    vmem = pl.BlockSpec(memory_space=pltpu.VMEM)

    def call(*args):
        return pl.pallas_call(
            kernel,
            out_shape=[jax.ShapeDtypeStruct(o, jnp.float32) for o in outs],
            in_specs=[vmem] * len(args),
            out_specs=[vmem] * len(outs),
            scratch_shapes=[pltpu.VMEM(s, jnp.float32) for s in scratch] + [pltpu.VMEM(s, jnp.bfloat16) for s in halves],
            compiler_params=pltpu.CompilerParams(vmem_limit_bytes=limit),
            cost_estimate=pl.CostEstimate(flops=flops, bytes_accessed=1 << 20, transcendentals=0),
        )(*args)

    return call


def body(factors, covariance, noise, positions):
    height, width = covariance.shape
    even = lax.axis_index("col") % 2 == 0

    head, tail = covariance[:, : 2 * B], covariance[:, width - 2 * B :]
    first = swap_cols(jnp.where(even, tail, head), False)
    second = swap_cols(jnp.where(even, head, tail), True)
    outer = (2 * B, width + 4 * B)
    send_a, send_b = local(edges_kernel, [outer, outer], limit=12 << 20)(covariance, first, second)
    outer_a = swap_rows(send_a, False)
    outer_b = swap_rows(send_b, True)

    base, edge_a, edge_b = local(spread_kernel, [(14 * T, B), (T, B), (T, B)], limit=4 << 20)(factors)
    edge_a = swap_rows(edge_a, False)
    edge_b = swap_rows(edge_b, True)
    own, keep, send = local(halves_kernel, [(14 * T, B), (8 * T, B), (8 * T, B)], limit=4 << 20)(base, edge_a, edge_b)

    far = jnp.stack([own] + [shift_z(own, -d) for d in FAR[1:]])

    turned = turn(jnp.stack([keep, flip_xl(send)]))
    turned = jnp.concatenate([turned, flip_row(turned, CORE)])
    turned = jnp.concatenate([turned, flip_row(turned, XH * CORE)])
    mine = jnp.concatenate([turned, fold_y(turned)])
    other = flip_row(mine, 1)

    near = [shift_near(far, -NEAR[1]), shift_near(far, -NEAR[2])]
    last = shift_near(near[0], -NEAR[1])
    near = jnp.concatenate(near)
    cross, cross_near, cross_last = (flip_xl(x) for x in (far, near, last))

    tall = (height + 4 * B, width)
    (moved,) = local(right_kernel, [tall], [(8, 3 * B, B)], 3000000000, 28 << 20, [(4 * B, 5 * B)] * 2)(
        mine, other, covariance, first, second, outer_a, outer_b
    )
    (early,) = local(gather_kernel, [(14, 3 * B, B)], flops=1000000, limit=12 << 20)(far, near, last, cross)
    (out,) = local(left_kernel, [(height, width)], [(14, 3 * B, B)], 2000000000, 28 << 20, [(8 * B, width)] * 2)(
        early, cross_near, cross_last, moved, noise, positions.reshape(-1, B)
    )
    return out


def solution(mesh):
    placed = (P(None, "row", "col"), P("row", "col"), P("row", "col"), P())
    return jax.shard_map(body, mesh=mesh, in_specs=placed, out_specs=P("row", "col"), check_vma=False)
```

```python
import jax
import jax.numpy as jnp
from jax import lax
from jax.experimental import pallas as pl
from jax.experimental.pallas import tpu as pltpu
from jax.sharding import PartitionSpec as P

B = 128
T = 12
XL, Z = 2, 16
Y, XH, CORE = 4, 2, 2
ROWS, COLS = Y * XH * CORE, XL * Z
BOTH = ("row", "col")
FAR = (0, -4, 4, 8)
NEAR = (0, -1, 1, -2)


def move(x, target):
    pairs = []
    for r in range(ROWS):
        for c in range(COLS):
            to = target(r, c)
            if to is not None:
                pairs.append((r * COLS + c, to[0] * COLS + to[1]))
    return lax.ppermute(x, BOTH, pairs)


def odd_pair(i, count):
    j = i + 1 if i % 2 else i - 1
    return j if 0 <= j < count else None


def swap_rows(x, odd):
    def target(r, c):
        to = odd_pair(r, ROWS) if odd else r ^ 1
        return None if to is None else (to, c)

    return move(x, target)


def swap_cols(x, odd):
    def target(r, c):
        to = odd_pair(c, COLS) if odd else c ^ 1
        return None if to is None else (r, to)

    return move(x, target)


def shift_z(x, d):
    return move(x, lambda r, c: (r, c // Z * Z + (c % Z + d) % Z))


def shift_near(x, d):
    return move(x, lambda r, c: (r, c // Z * Z + (c % Z + (d if r % 2 == 0 else -d)) % Z))


def fold_y(x):
    return move(x, lambda r, c: (r ^ (Y - 1) * XH * CORE, c))


def flip_row(x, bit):
    return move(x, lambda r, c: (r ^ bit, c))


def flip_xl(x):
    return move(x, lambda r, c: (r, (c + Z) % COLS))


def turn(x):
    def target(r, c):
        xl, z = divmod(c, Z)
        return (z % Y * XH + z // Y % XH) * CORE + z // (Y * XH), 2 * r + xl

    return move(x, target)


def split(x):
    hi = x.astype(jnp.bfloat16)
    return hi, (x - hi.astype(jnp.float32)).astype(jnp.bfloat16)


def product(a, b, contract):
    dims = (contract, ((), ()))
    (ah, al), (bh, bl) = a, b
    out = lax.dot_general(al, bh, dims, preferred_element_type=jnp.float32)
    out += lax.dot_general(ah, bl, dims, preferred_element_type=jnp.float32)
    return out + lax.dot_general(ah, bh, dims, preferred_element_type=jnp.float32)


def wide(ref, q):
    return jnp.concatenate([ref[q, k * B : (k + 1) * B, :] for k in range(3)], axis=1)


def band(ref, q, count):
    if count == 1:
        return split(wide(ref, q))
    zero = jnp.zeros((B, B), jnp.float32)
    upper = jnp.concatenate([wide(ref, q), zero], axis=1)
    lower = jnp.concatenate([zero, wide(ref, q + 1)], axis=1)
    return split(jnp.concatenate([upper, lower], axis=0))


def place(held, piece, slot, at, count):
    start = pl.multiple_of(at * T, 4)
    for q in range(count):
        held[q, pl.ds(start, T), :] = piece[slot, q * T : (q + 1) * T, :]


def spread_kernel(factors, base, first, second):
    core = lax.axis_index("row") % 2
    base[0:T, :] = jnp.zeros((T, B), jnp.float32)
    base[7 * T : 8 * T, :] = jnp.zeros((T, B), jnp.float32)
    for f, at in ((0, 1), (1, 8)):
        for t in range(T):
            base[pl.ds(at * T + t, 6, stride=T), :] = factors[f, :, t * B : (t + 1) * B]
    top, bottom = base[T : 2 * T, :], base[6 * T : 7 * T, :]

    @pl.when(core == 0)
    def _():
        first[...] = bottom
        second[...] = top

    @pl.when(core == 1)
    def _():
        first[...] = top
        second[...] = bottom


def halves_kernel(base, first, second, own, keep, send):
    core, odd = lax.axis_index("row") % 2, lax.axis_index("col") // Z
    own[...] = base[...]

    @pl.when(core == 0)
    def _():
        own[0:T, :] = second[...]
        own[7 * T : 8 * T, :] = first[...]

    @pl.when(core == 1)
    def _():
        own[0:T, :] = first[...]
        own[7 * T : 8 * T, :] = second[...]

    def half(h, out):
        out[0 : 5 * T, :] = own[3 * h * T : (3 * h + 5) * T, :]
        out[5 * T : 8 * T, :] = own[(8 + 3 * h) * T : (11 + 3 * h) * T, :]

    @pl.when(odd == 0)
    def _():
        half(0, keep)
        half(1, send)

    @pl.when(odd == 1)
    def _():
        half(1, keep)
        half(0, send)


def extend_kernel(tile, first, second, out, send_a, send_b):
    core, odd = lax.axis_index("row") % 2, lax.axis_index("col") % 2
    height, width = tile.shape
    out[2 * B : 2 * B + height, :] = tile[...]

    @pl.when(core == 0)
    def _():
        out[: 2 * B, :] = second[...]
        out[2 * B + height :, :] = first[...]

    @pl.when(core == 1)
    def _():
        out[: 2 * B, :] = first[...]
        out[2 * B + height :, :] = second[...]

    @pl.when(odd == 0)
    def _():
        send_a[...] = out[:, width - 2 * B :]
        send_b[...] = out[:, : 2 * B]

    @pl.when(odd == 1)
    def _():
        send_a[...] = out[:, : 2 * B]
        send_b[...] = out[:, width - 2 * B :]


def right_kernel(mine, other, tile, first, second, out, held, high, low):
    row, c = lax.axis_index("row"), lax.axis_index("col")
    y, xh, core = row // (XH * CORE), (row // CORE) % XH, row % CORE
    odd = c % 2
    for source, k in ((mine, core), (other, 1 - core)):
        for i, bits in enumerate((0, 1, 3, 2)):
            for e, x in enumerate((xh, 1 - xh)):
                at = (y ^ bits) + Y * x + Y * XH * k
                place(held, source, i * 4 + e * 2, at + Z * odd, 8)
                place(held, source, i * 4 + e * 2 + 1, at + Z * (1 - odd), 8)
    even = odd == 0
    half = out.shape[0] // 2
    for part in range(2):
        rows = slice(part * half, (part + 1) * half)
        before = jnp.where(even, second[rows, :], first[rows, :])
        after = jnp.where(even, first[rows, :], second[rows, :])
        hi, lo = split(jnp.concatenate([before, tile[rows, :], after], axis=1))
        for j, n in ((0, 2), (2, 2), (4, 1)):
            window = slice(j * B, (j + n + 2) * B)
            total = product((hi[:, window], lo[:, window]), band(held, j, n), ((1,), (1,)))
            columns = slice(j * B, (j + n) * B)
            high[:, columns], low[:, columns] = split(total)
        for j, n in ((0, 2), (2, 1)):
            window = slice(j * B, (j + n + 2) * B)
            total = product((high[:, window], low[:, window]), band(held, 5 + j, n), ((1,), (1,)))
            out[rows, j * B : (j + n) * B] = total


def place_near(held, piece, slot, xl, near):
    core, z = lax.axis_index("row") % 2, lax.axis_index("col") % Z
    for j, far in enumerate(FAR):
        at = xl * Z + (z + (1 - 2 * core) * near + far + Z) % Z
        place(held, piece, slot + j, at, 14)


def gather_kernel(far, near, last, cross, held):
    xl = lax.axis_index("col") // Z
    place_near(held, far, 0, xl, NEAR[0])
    place_near(held, near, 0, xl, NEAR[1])
    place_near(held, near, 4, xl, NEAR[2])
    place_near(held, last, 0, xl, NEAR[3])
    place_near(held, cross, 0, 1 - xl, NEAR[0])


def left_kernel(early, cross, last, whole, noise, places, out, held, high, low):
    row, col = lax.axis_index("row"), lax.axis_index("col")
    xl = col // Z
    held[...] = early[...]
    place_near(held, cross, 0, 1 - xl, NEAR[1])
    place_near(held, cross, 4, 1 - xl, NEAR[2])
    place_near(held, last, 0, 1 - xl, NEAR[3])
    whole_high, whole_low = split(whole[...])
    for i in range(0, 8, 2):
        window = slice(i * B, (i + 4) * B)
        total = product(band(held, i, 2), (whole_high[window, :], whole_low[window, :]), ((1,), (0,)))
        rows = slice(i * B, (i + 2) * B)
        high[rows, :], low[rows, :] = split(total)
    across = jnp.concatenate([places[pl.ds(col * 3 + j, 1), :] for j in range(3)], axis=1)
    for i in range(0, 6, 2):
        rows = slice(i * B, (i + 2) * B)
        window = slice(i * B, (i + 4) * B)
        total = product(band(held, 8 + i, 2), (high[window, :], low[window, :]), ((1,), (0,)))
        down = [jnp.transpose(jnp.broadcast_to(places[pl.ds(row * 6 + i + k, 1), :], (B, B))) for k in range(2)]
        down = jnp.concatenate([jnp.concatenate(down, axis=0)] * 3, axis=1)
        distance = (down - across) / 0.5
        out[rows, :] = total * jnp.exp(-distance * distance) + noise[rows, :]


def local(kernel, outs, scratch=(), flops=0, limit=None, halves=()):
    vmem = pl.BlockSpec(memory_space=pltpu.VMEM)

    def call(*args):
        return pl.pallas_call(
            kernel,
            out_shape=[jax.ShapeDtypeStruct(o, jnp.float32) for o in outs],
            in_specs=[vmem] * len(args),
            out_specs=[vmem] * len(outs),
            scratch_shapes=[pltpu.VMEM(s, jnp.float32) for s in scratch] + [pltpu.VMEM(s, jnp.bfloat16) for s in halves],
            compiler_params=pltpu.CompilerParams(vmem_limit_bytes=limit),
            cost_estimate=pl.CostEstimate(flops=flops, bytes_accessed=1 << 20, transcendentals=0),
        )(*args)

    return call


def body(factors, covariance, noise, positions):
    height, width = covariance.shape
    above = lax.axis_index("row") % 2 == 0

    head, tail = covariance[: 2 * B], covariance[height - 2 * B :]
    first = swap_rows(jnp.where(above, tail, head), False)
    second = swap_rows(jnp.where(above, head, tail), True)
    tall, sides = (height + 4 * B, width), (height + 4 * B, 2 * B)
    tile, send_a, send_b = local(extend_kernel, [tall, sides, sides], limit=12 << 20)(covariance, first, second)
    first = swap_cols(send_a, False)
    second = swap_cols(send_b, True)

    base, edge_a, edge_b = local(spread_kernel, [(14 * T, B), (T, B), (T, B)], limit=4 << 20)(factors)
    edge_a = swap_rows(edge_a, False)
    edge_b = swap_rows(edge_b, True)
    own, keep, send = local(halves_kernel, [(14 * T, B), (8 * T, B), (8 * T, B)], limit=4 << 20)(base, edge_a, edge_b)

    far = jnp.stack([own] + [shift_z(own, -d) for d in FAR[1:]])

    turned = turn(jnp.stack([keep, flip_xl(send)]))
    turned = jnp.concatenate([turned, flip_row(turned, CORE)])
    turned = jnp.concatenate([turned, flip_row(turned, XH * CORE)])
    mine = jnp.concatenate([turned, fold_y(turned)])
    other = flip_row(mine, 1)

    near = [shift_near(far, -NEAR[1]), shift_near(far, -NEAR[2])]
    last = shift_near(near[0], -NEAR[1])
    near = jnp.concatenate(near)
    cross, cross_near, cross_last = (flip_xl(x) for x in (far, near, last))

    (moved,) = local(right_kernel, [tall], [(8, 3 * B, B)], 3000000000, 28 << 20, [(tall[0] // 2, 5 * B)] * 2)(
        mine, other, tile, first, second
    )
    (early,) = local(gather_kernel, [(14, 3 * B, B)], flops=1000000, limit=12 << 20)(far, near, last, cross)
    (out,) = local(left_kernel, [(height, width)], [(14, 3 * B, B)], 2000000000, 28 << 20, [(8 * B, width)] * 2)(
        early, cross_near, cross_last, moved, noise, positions.reshape(-1, B)
    )
    return out


def solution(mesh):
    placed = (P(None, "row", "col"), P("row", "col"), P("row", "col"), P())
    return jax.shard_map(body, mesh=mesh, in_specs=placed, out_specs=P("row", "col"), check_vma=False)
```
